32 devices in a mesh: grp: 2 (over y), seq: 4 (over z), fsdp: 2 (over x), head: 2 (over core).
Axes of the slice: x: 2, y: 2, z: 4, core: 2. Of those that a mesh axis runs over, the one named last changes fastest.
Arguments:
- tokens: bfloat16 [6144, 3072], P(('grp', 'seq'), 'head'), parts along dimension 0
- qkv_weight: bfloat16 [3072, 1536], P('fsdp', 'head'), may hold values from -0.109375 to 0.109375
- shift_mod: float32 [6144], P('grp'), parts along dimension 0, may hold values from -3 to 3
- scale_mod: float32 [6144], P('grp'), parts along dimension 0, may hold values from -2 to 2
- q_gain: float32 [4, 128], P(('fsdp', 'head'))
- k_gain: float32 [4, 128], P(('fsdp', 'head'))
- cached: bfloat16 [6144, 512], P(('grp', 'seq'), ('fsdp', 'head')), parts along dimension 0, may hold values from -6 to 6
- active: int32 [48], P(('grp', 'seq')), parts along dimension 0, may hold values from -1 to 5, as said below
- cache_slot: int32 [48], P(('grp', 'seq')), parts along dimension 0, may hold values from 0 to 5, as said below
Outputs:
- blended: bfloat16 [6144, 512], P(('grp', 'seq'), ('fsdp', 'head')), parts along dimension 0
The draws below stay inside these ranges and needn't reach their ends.
There are 2 independent parts, one for each index of `grp`. The reference program is written for one: setup_inputs(seed, part) draws one part's arguments, and reference() takes and returns one part's arrays. A program takes and returns all parts, laid end to end along the dimension named above; an argument that names none is the same for every part. Nothing has to cross between parts.
Inputs may be any that keep to these rules, and one draw needn't show every extreme that they name: Entries s * 6 to s * 6 + 5 list the active local blocks of index s of seq in rising order, each at most once, followed by -1 for the rest. Over the whole sequence exactly 12 blocks are active; some index of seq has all 6 blocks active and some has none. `cache_slot`: entries s * 6 to s * 6 + 5 are a permutation of 0 to 5.
All inputs are finite; a program needn't handle non-finite values.
Results may differ from the reference program's by a relative error of at most 0.012.
The reference program's roundings to bfloat16 on the way count: a program that leaves them out, or rounds other values in their place, can miss the bound.
Values may be sent and summed in bfloat16 or wider, within the bound.
No kernel may reach another device: no remote copies, remote signals or barrier semaphores. Data moves between devices by JAX's collectives and lax.ppermute only.
A program may use at most 64 MiB of HBM per device.

```python
import math
import jax
import jax.numpy as jnp
from jax import lax

D = 3072
HD = 128
QBLK = 128
H = 4
TOKENS = 3072
BLK = 6
NBLK = 24
N_SEQ = 4
N_FSDP = 2
N_HEAD = 2


def draw_tokens(key, part):
    key_base = jax.random.fold_in(key, 11)
    key_rows = jax.random.fold_in(key, 12)
    key_cols = jax.random.fold_in(key, 13)
    row_scale = jnp.exp(jax.random.uniform(key_rows, (TOKENS, 1), jnp.float32, 0.0, math.log(10.0)))
    col_scale = jnp.exp(jax.random.uniform(key_cols, (1, D), jnp.float32, 0.0, math.log(10.0)))
    base_vals = jax.random.normal(key_base, (TOKENS, D), jnp.float32)
    return (base_vals * row_scale * col_scale * 0.25).astype(jnp.bfloat16)


def head_gains(key, salt):
    own_key = jax.random.fold_in(key, salt)
    return jnp.exp(jax.random.uniform(own_key, (H, HD), jnp.float32, math.log(1.0), math.log(3.0)))


def draw_q_gain(key, part):
    return head_gains(key, 31)


def draw_k_gain(key, part):
    return head_gains(key, 32)


def draw_active(key, part):
    key_count = jax.random.fold_in(key, 41)
    key_order = jax.random.fold_in(key, 42)
    key_pick = jax.random.fold_in(key, 43)
    half_count = N_SEQ // 2
    paired = jax.random.randint(key_count, (half_count,), 0, BLK + 1)
    paired = paired.at[0].set(BLK)
    both_sides = jnp.concatenate([paired, BLK - paired])
    order_ids = jax.random.permutation(key_order, N_SEQ)
    counts = both_sides[order_ids]
    local_ids = jnp.arange(BLK, dtype=jnp.int32)
    scores = jax.random.randint(key_pick, (N_SEQ, BLK), 0, 1 << 20) * BLK + local_ids[None, :]
    ranks = jnp.argsort(jnp.argsort(scores, axis=1), axis=1)
    chosen = ranks < counts[:, None]
    listed = jnp.sort(jnp.where(chosen, local_ids[None, :], BLK), axis=1)
    return jnp.where(listed < BLK, listed, -1).reshape(NBLK).astype(jnp.int32)


def draw_cache_slot(key, part):
    local_ids = jnp.arange(BLK, dtype=jnp.int32)
    scores = jax.random.randint(jax.random.fold_in(key, 51), (N_SEQ, BLK), 0, 1 << 20) * BLK + local_ids[None, :]
    return jnp.argsort(scores, axis=1).reshape(NBLK).astype(jnp.int32)


def levels(key, shape, shards, least, largest):
    level, own = 1.0, jax.random.fold_in(key, 6)
    for axis_at, shards_of in shards:
        steps = jnp.exp(jax.random.uniform(jax.random.fold_in(own, axis_at), (shards_of,), jnp.float32, least / len(shards), largest / len(shards)))
        level = level * jnp.repeat(steps, shape[axis_at] // shards_of).reshape([-1 if axis == axis_at else 1 for axis in range(len(shape))])
    return level


def normal_values(key, dims, width, reach, shards=(), held_as=jnp.bfloat16):
    factor_of = levels(key, dims, shards, -0.22, 0.18) if shards else 1.0
    array = jax.random.normal(key, dims, jnp.float32) * width * factor_of
    return jnp.minimum(jnp.maximum(array, -reach), reach).astype(held_as)


def setup_inputs(seed: int = 0, part: int = 0) -> dict:
    arg_keys = jax.random.split(jax.random.key(seed), 10)
    own_keys = jax.random.split(jax.random.fold_in(arg_keys[9], part), 10)
    tokens = draw_tokens(jax.random.fold_in(jax.random.fold_in(arg_keys[9], part), 71), part)
    qkv_weight = normal_values(arg_keys[1], (D, 3 * H * HD), D ** -0.5, 0.109375, ((0, 2), (1, 2)))
    shift_mod = normal_values(own_keys[2], (D,), 0.5, 3.0, (), jnp.float32)
    scale_mod = normal_values(own_keys[3], (D,), 0.3, 2.0, (), jnp.float32)
    q_gain = draw_q_gain(jax.random.fold_in(arg_keys[9], 71), part)
    k_gain = draw_k_gain(jax.random.fold_in(arg_keys[9], 71), part)
    cached = normal_values(own_keys[6], (TOKENS, H * HD), 1.0, 6.0, ((0, 4), (1, 4)))
    active = draw_active(jax.random.fold_in(jax.random.fold_in(arg_keys[9], part), 71), part)
    cache_slot = draw_cache_slot(jax.random.fold_in(jax.random.fold_in(arg_keys[9], part), 71), part)
    return {"tokens": tokens, "qkv_weight": qkv_weight, "shift_mod": shift_mod, "scale_mod": scale_mod, "q_gain": q_gain, "k_gain": k_gain, "cached": cached, "active": active, "cache_slot": cache_slot}


eps_norm = 1e-06

def rms_scaled(vector, gain_row):
    return vector * lax.rsqrt(lax.optimization_barrier(jnp.mean(vector * vector, axis=-1, keepdims=True)) + eps_norm) * gain_row

def reference(tokens, qkv_weight, shift_mod, scale_mod, q_gain, k_gain, cached, active, cache_slot):
    gathered = tokens.astype(jnp.float32)
    row_mean = lax.optimization_barrier(jnp.mean(gathered, axis=1, keepdims=True))
    centred = gathered - row_mean
    row_var = lax.optimization_barrier(jnp.mean(centred * centred, axis=1, keepdims=True))
    normed = (centred * lax.rsqrt(row_var + eps_norm) * (1.0 + scale_mod) + shift_mod).astype(jnp.bfloat16)
    arranged = qkv_weight.reshape(D, N_HEAD, N_FSDP, 3, HD).transpose(0, 2, 1, 3, 4).reshape(D, 3 * H * HD)
    projected = jnp.dot(normed, arranged, preferred_element_type=jnp.float32).reshape(TOKENS, H, 3, HD)
    queries = rms_scaled(projected[:, :, 0], q_gain[None]).astype(jnp.bfloat16)
    key_half = rms_scaled(projected[:, :, 1], k_gain[None]).astype(jnp.bfloat16)
    value_half = projected[:, :, 2].astype(jnp.bfloat16)
    key_full = lax.optimization_barrier(key_half).astype(jnp.float32)
    value_full = lax.optimization_barrier(value_half).astype(jnp.float32)
    live_mask = active >= 0
    device_ids = (jnp.arange(NBLK, dtype=jnp.int32) // BLK).astype(jnp.int32)
    global_block = (device_ids * BLK + jnp.where(live_mask, active, 0)).astype(jnp.int32)
    picked = jnp.nonzero(live_mask, size=NBLK // 2)[0].astype(jnp.int32)
    targets = global_block[picked].astype(jnp.int32)

    def one_block(block_id):
        start_row = (block_id * QBLK).astype(jnp.int32)
        query_block = lax.dynamic_slice_in_dim(queries, start_row, QBLK, 0)
        query_full = lax.optimization_barrier(query_block).astype(jnp.float32)
        scores = jnp.einsum('qhd,khd->hqk', query_full, key_full) * HD ** (-0.5)
        peak = lax.optimization_barrier(jnp.max(scores, axis=2, keepdims=True))
        weights = jnp.exp(scores - peak)
        probs = lax.optimization_barrier(weights.astype(jnp.bfloat16)).astype(jnp.float32)
        totals = lax.optimization_barrier(jnp.sum(weights, axis=2)).T
        mixed = jnp.einsum('hqk,khd->qhd', probs, value_full) / totals[:, :, None]
        return mixed.astype(jnp.bfloat16).reshape(QBLK, H * HD)
    fresh_rows = lax.map(one_block, targets)
    stale_rows = cached.reshape(NBLK, QBLK, H * HD)[(device_ids * BLK + cache_slot).astype(jnp.int32)]
    return stale_rows.at[targets].set(fresh_rows).reshape(TOKENS, H * HD)
```

```python
import functools

import jax
import jax.numpy as jnp
from jax import lax
from jax.experimental import pallas as pl
from jax.experimental.pallas import tpu as pltpu
from jax.sharding import PartitionSpec as P


eps_norm = 1e-06
VMEM = pl.BlockSpec(memory_space=pltpu.VMEM)
SMEM = pl.BlockSpec(memory_space=pltpu.SMEM)
ANY = pl.BlockSpec(memory_space=pl.ANY)


def rms_scaled(vector, gain_row):
    return (
        vector * lax.rsqrt(jnp.mean(vector * vector, axis=-1, keepdims=True) + eps_norm) * gain_row
    )


def call(body, out, ins, flops, scalars=0, scratch=(), limit=16 << 20):
    nbytes = sum(x.size * x.dtype.itemsize for x in ins)
    many = isinstance(out, tuple)
    return pl.pallas_call(
        body,
        out_shape=out,
        in_specs=[SMEM] * scalars + [VMEM] * (len(ins) - scalars),
        out_specs=(VMEM,) * len(out) if many else VMEM,
        scratch_shapes=scratch,
        compiler_params=pltpu.CompilerParams(vmem_limit_bytes=limit),
        cost_estimate=pl.CostEstimate(flops=flops, bytes_accessed=nbytes, transcendentals=0),
    )(*ins)


def shape(dims, dtype):
    return jax.ShapeDtypeStruct(dims, dtype)


def tile_rows(index, tile):
    return pl.ds(pl.multiple_of(index * tile, tile), tile)


def half_moments(values):
    mean = jnp.mean(values, axis=1, keepdims=True)
    centred = values - mean
    return mean, jnp.sum(centred * centred, axis=1, keepdims=True)


def moments_kernel(own_ref, out_ref):
    mean, square = half_moments(own_ref[...].astype(jnp.float32))
    out_ref[...] = jnp.concatenate([mean, square], axis=1)


def moments(own):
    rows, half = own.shape
    tile = rows // 6
    return pl.pallas_call(
        moments_kernel,
        out_shape=shape((rows, 2), jnp.float32),
        grid=(rows // tile,),
        in_specs=[pl.BlockSpec((tile, half), lambda at: (at, 0))],
        out_specs=pl.BlockSpec((tile, 2), lambda at: (at, 0)),
        compiler_params=pltpu.CompilerParams(vmem_limit_bytes=8 << 20),
        cost_estimate=pl.CostEstimate(
            flops=5 * rows * half, bytes_accessed=2 * rows * half, transcendentals=0
        ),
        name="moments",
    )(own)


def columns_of(block, head_dim, parts):
    return pl.ds(pl.multiple_of(block * head_dim, head_dim), parts * head_dim)


def normalise_kernel(tile, second, own_ref, other_ref, near_ref, far_ref, weight_ref, scale_ref,
                     shift_ref, *refs):
    half = own_ref.shape[1]
    head_dim = weight_ref.shape[1] // 6
    mine = lax.axis_index("fsdp")
    matched = mine == lax.axis_index("head")
    take_own = jnp.logical_not(matched) if second else matched
    features = pl.ds(pl.multiple_of((1 - mine if second else mine) * half, half), half)
    scale = 1.0 + scale_ref[:, features]
    shift = shift_ref[:, features]
    if second:
        weight = weight_ref[:, columns_of(3 * mine + 1, head_dim, 1)]
    else:
        weight = jnp.concatenate(
            [
                weight_ref[:, columns_of(3 * (1 - mine), head_dim, 1)],
                weight_ref[:, columns_of(3 * (1 - mine) + 2, head_dim, 1)],
            ],
            axis=1,
        )
    for start in range(0, own_ref.shape[0], tile):
        rows = slice(start, start + tile)
        near_mean, far_mean = near_ref[rows, 0:1], far_ref[rows, 0:1]
        mean = 0.5 * (near_mean + far_mean)
        apart = 0.5 * (near_mean - far_mean)
        var = (near_ref[rows, 1:2] + far_ref[rows, 1:2]) / (2 * half) + apart * apart
        factor = lax.rsqrt(var + eps_norm)
        values = jnp.where(take_own, own_ref[rows, :], other_ref[rows, :]).astype(jnp.float32)
        normed = ((values - mean) * factor * scale + shift).astype(jnp.bfloat16)
        if second:
            first_ref, normed_ref, key_ref = refs
            normed_ref[rows, :] = normed
            key_ref[rows, :] = jnp.dot(
                first_ref[rows, :], weight, preferred_element_type=jnp.float32
            )
        else:
            normed_ref, query_ref, value_ref = refs
            normed_ref[rows, :] = normed
            sums = jnp.dot(normed, weight, preferred_element_type=jnp.float32)
            query_ref[rows, :] = sums[:, :head_dim].astype(query_ref.dtype)
            value_ref[rows, :] = sums[:, head_dim:].astype(value_ref.dtype)


def normalise(own, other, near, far, weight, scale, shift, head_dim, first=None):
    rows, half = own.shape
    second = first is not None
    if second:
        outs = (shape((rows, head_dim), jnp.float32),)
    else:
        outs = (shape((rows, head_dim), jnp.bfloat16),) * 2
    operands = (own, other, near, far, weight, scale, shift) + ((first,) if second else ())
    return call(
        functools.partial(normalise_kernel, rows // 3, second),
        (shape((rows, half), jnp.bfloat16), *outs), operands,
        (2 if second else 4) * rows * half * head_dim,
    )


def project_kernel(normed_ref, weight_ref, query_ref, value_ref):
    head_dim = query_ref.shape[1]
    mine = lax.axis_index("fsdp")
    weight = jnp.concatenate(
        [
            weight_ref[:, columns_of(3 * mine, head_dim, 1)],
            weight_ref[:, columns_of(3 * mine + 2, head_dim, 1)],
        ],
        axis=1,
    )
    sums = jnp.dot(normed_ref[...], weight, preferred_element_type=jnp.float32)
    query_ref[...] = sums[:, :head_dim]
    value_ref[...] = sums[:, head_dim:]


def project(normed, weight, head_dim):
    rows, half = normed.shape
    return call(
        project_kernel, (shape((rows, head_dim), jnp.float32),) * 2, (normed, weight),
        4 * rows * half * head_dim,
    )


def foreign_keys_kernel(weight_ref, out_ref, sem_ref):
    head_dim = out_ref.shape[1]
    cols = columns_of(3 * (1 - lax.axis_index("fsdp")) + 1, head_dim, 1)
    copy = pltpu.make_async_copy(weight_ref.at[:, cols], out_ref, sem_ref)
    copy.start()
    copy.wait()


def foreign_keys(weight, head_dim):
    rows = weight.shape[0]
    return pl.pallas_call(
        foreign_keys_kernel,
        out_shape=shape((rows, head_dim), weight.dtype),
        in_specs=[ANY],
        out_specs=VMEM,
        scratch_shapes=[pltpu.SemaphoreType.DMA],
        compiler_params=pltpu.CompilerParams(vmem_limit_bytes=2 << 20),
        cost_estimate=pl.CostEstimate(
            flops=0, bytes_accessed=4 * rows * head_dim, transcendentals=0
        ),
        name="foreign_keys",
    )(pltpu.with_memory_space_constraint(weight, pltpu.HBM))


def keys_kernel(kept_ref, normed_ref, weight_ref, gain_ref, out_ref):
    key = kept_ref[...] + jnp.dot(
        normed_ref[...], weight_ref[...], preferred_element_type=jnp.float32
    )
    out_ref[...] = rms_scaled(key, gain_ref[...]).astype(out_ref.dtype)


def finish_keys(kept, normed, weight, gain):
    rows, head_dim = kept.shape[0], gain.shape[1]
    return call(
        keys_kernel, shape((rows, head_dim), jnp.bfloat16), (kept, normed, weight, gain),
        2 * normed.size * head_dim,
    )


def finish_kernel(part, kept_ref, got_ref, gain_ref, out_ref):
    row = kept_ref[...] + got_ref[...].astype(jnp.float32)
    if part < 2:
        out_ref[...] = rms_scaled(row, gain_ref[...]).astype(out_ref.dtype)
    else:
        out_ref[...] = row.T.astype(out_ref.dtype)


def finish(part, kept, got, gain):
    dims = got.shape if part < 2 else got.shape[::-1]
    return call(
        functools.partial(finish_kernel, part), shape(dims, jnp.bfloat16), (kept, got, gain),
        10 * got.size,
    )


def attend_kernel(blocks, spans, stage, listed, *refs):
    if listed:
        active_ref, refs = refs[0], refs[1:]
    query_ref, refs = refs[0], refs[1:]
    span_refs, refs = refs[: 2 * spans], refs[2 * spans :]
    if stage == "close":
        given, given_mixed, stats_ref, mixed_ref = refs
    else:
        stats_ref, mixed_ref = refs
    head_dim = query_ref.shape[1]
    width = 2 * query_ref.shape[0] // blocks
    factor = head_dim ** (-0.5) * 1.4426950408889634

    def pair(index):
        cols = slice(index * width, (index + 1) * width)
        queries = query_ref[cols, :]
        if stage == "close":
            top, total, mixed = given[0:1, cols], given[1:2, cols], given_mixed[:, cols]
        for at in range(spans):
            key_ref, value_ref = span_refs[2 * at], span_refs[2 * at + 1]
            scores = lax.dot_general(
                key_ref[...], queries, (((1,), (1,)), ((), ())),
                preferred_element_type=jnp.float32,
            )
            best = jnp.max(scores, axis=0, keepdims=True)
            first = at == 0 and stage != "close"
            new_top = best if first else jnp.maximum(top, best)
            weights = jnp.exp2((scores - new_top) * factor)
            added = jnp.sum(weights, axis=0, keepdims=True)
            product = jnp.dot(
                value_ref[...], weights.astype(jnp.bfloat16), preferred_element_type=jnp.float32
            )
            if first:
                total, mixed = added, product
            else:
                shrink = jnp.exp2((top - new_top) * factor)
                total, mixed = total * shrink + added, mixed * shrink + product
            top = new_top
        stats_ref[0:1, cols] = top
        stats_ref[1:2, cols] = total
        mixed_ref[:, cols] = (mixed if stage == "open" else mixed / total).astype(mixed_ref.dtype)

    for index in range(blocks // 2):
        if listed:
            here = [
                (active_ref[at] == 2 * index) | (active_ref[at] == 2 * index + 1)
                for at in range(blocks)
            ]
            pl.when(functools.reduce(jnp.logical_or, here))(functools.partial(pair, index))
        else:
            pair(index)


def attend(blocks, queries, spans, stage, dtype, state=(), active=None):
    rows, head_dim = queries.shape
    listed = () if active is None else (active,)
    flat = [x for span in spans for x in span]
    return call(
        functools.partial(attend_kernel, blocks, len(spans), stage, bool(listed)),
        (shape((8, rows), jnp.float32), shape((head_dim, rows), dtype)),
        (*listed, queries, *flat, *state),
        4 * queries.size * sum(span[0].shape[0] for span in spans),
        scalars=len(listed),
    )


def peek_kernel(blocks, query_ref, key_ref, given_ref, stats_ref, weights_ref):
    head_dim = query_ref.shape[1]
    width = 2 * query_ref.shape[0] // blocks
    factor = head_dim ** (-0.5) * 1.4426950408889634
    for index in range(blocks // 2):
        cols = slice(index * width, (index + 1) * width)
        scores = lax.dot_general(
            key_ref[...], query_ref[cols, :], (((1,), (1,)), ((), ())),
            preferred_element_type=jnp.float32,
        )
        top = given_ref[0:1, cols]
        new_top = jnp.maximum(top, jnp.max(scores, axis=0, keepdims=True))
        weights = jnp.exp2((scores - new_top) * factor)
        shrink = jnp.exp2((top - new_top) * factor)
        stats_ref[0:1, cols] = new_top
        stats_ref[1:2, cols] = given_ref[1:2, cols] * shrink + jnp.sum(
            weights, axis=0, keepdims=True
        )
        stats_ref[2:3, cols] = shrink
        weights_ref[:, cols] = weights.astype(jnp.bfloat16)


def peek(blocks, queries, keys, given):
    return call(
        functools.partial(peek_kernel, blocks),
        (shape(given.shape, jnp.float32), shape((keys.shape[0], queries.shape[0]), jnp.bfloat16)),
        (queries, keys, given), 2 * queries.size * keys.shape[0],
    )


def close_kernel(stats_ref, weights_ref, value_ref, mixed_ref, out_ref):
    product = jnp.dot(value_ref[...], weights_ref[...], preferred_element_type=jnp.float32)
    out_ref[...] = (
        (mixed_ref[...] * stats_ref[2:3, :] + product) / stats_ref[1:2, :]
    ).astype(out_ref.dtype)


def close(stats, weights, values, mixed):
    return call(
        close_kernel, shape(mixed.shape, jnp.bfloat16), (stats, weights, values, mixed),
        2 * values.size * weights.shape[1],
    )


def stale_kernel(blocks, active_ref, slot_ref, cached_ref, out_ref, fresh_ref):
    rows = cached_ref.shape[0] // blocks
    for block in range(blocks):
        here = functools.reduce(
            jnp.logical_or, [active_ref[at] == block for at in range(blocks)]
        )
        place = slice(block * rows, (block + 1) * rows)
        stale = cached_ref[tile_rows(slot_ref[block], rows), :]
        out_ref[place, :] = jnp.where(here, jnp.zeros_like(stale), stale)
        fresh_ref[:, place] = jnp.full((fresh_ref.shape[0], rows), jnp.where(here, 1.0, 0.0))


def stale_rows(active, slots, cached):
    return call(
        functools.partial(stale_kernel, active.shape[0]),
        (shape(cached.shape, cached.dtype), shape((8, cached.shape[0]), jnp.float32)),
        (active, slots, cached), 8 * cached.size, scalars=2,
    )


def blend_kernel(stale_ref, fresh_ref, *refs):
    out_ref = refs[-1]
    factor = out_ref.shape[1] ** (-0.5) * 1.4426950408889634
    stats, mixes = refs[0:-1:2], refs[1:-1:2]
    top = functools.reduce(jnp.maximum, [ref[0:1, :] for ref in stats])
    parts = [ref[1:2, :] * jnp.exp2((ref[0:1, :] - top) * factor) for ref in stats]
    total = functools.reduce(jnp.add, parts)
    mixed = functools.reduce(
        jnp.add, [ref[...].astype(jnp.float32) * (part / total) for ref, part in zip(mixes, parts)]
    )
    mixed = jnp.where(fresh_ref[0:1, :] > 0.5, mixed, 0.0)
    out_ref[...] = mixed.T.astype(out_ref.dtype) + stale_ref[...]


def blend(stale, fresh, shares):
    return call(
        blend_kernel, shape(stale.shape, stale.dtype),
        (stale, fresh, *[x for share in shares for x in share]), 8 * stale.size,
    )


def swapped_plan(tokens, qkv_weight, shift_mod, scale_mod, q_gain, k_gain, cached, active,
                 cache_slot):
    head_dim = q_gain.shape[1]
    blocks = active.shape[0]
    swap = [(0, 1), (1, 0)]
    beside = [(0, 1), (1, 0), (2, 3), (3, 2)]
    across = [(0, 2), (2, 0), (1, 3), (3, 1)]

    other = lax.ppermute(tokens, "head", swap)
    got_columns = lax.ppermute(foreign_keys(qkv_weight, head_dim), "fsdp", swap)
    near = moments(tokens)
    far = lax.ppermute(near, "head", swap)
    common = (
        tokens, other, near, far, qkv_weight,
        scale_mod.reshape(1, -1), shift_mod.reshape(1, -1), head_dim,
    )
    first, part_query, part_value = normalise(*common)
    got_query = lax.ppermute(part_query, "fsdp", swap)
    got_value = lax.ppermute(part_value, "fsdp", swap)
    second, kept_key = normalise(*common, first=first)

    keys = finish_keys(kept_key, second, got_columns, k_gain)
    beside_keys = lax.ppermute(keys, "seq", beside)
    kept_query, kept_value = project(first, qkv_weight, head_dim)
    queries = finish(0, kept_query, got_query, q_gain)
    visitors = lax.ppermute(queries, "seq", across)
    values = finish(2, kept_value, got_value, k_gain)
    beside_values = lax.ppermute(values, "seq", beside)

    stale, fresh = stale_rows(active, cache_slot, cached)
    stats, mixed = attend(blocks, visitors, [(keys, values)], "open", jnp.float32)
    stats, weights = peek(blocks, visitors, beside_keys, stats)
    lent = close(stats, weights, beside_values, mixed)
    returned = (lax.ppermute(stats, "seq", across), lax.ppermute(lent, "seq", across))
    spans = [(keys, values), (beside_keys, beside_values)]
    own = attend(blocks, queries, spans, "whole", jnp.float32, active=active)
    return blend(stale, fresh, [own, returned])


def gathered_plan(tokens, qkv_weight, shift_mod, scale_mod, q_gain, k_gain, cached, active,
                  cache_slot):
    gathered = lax.all_gather(tokens, "head", axis=1, tiled=True).astype(jnp.float32)
    row_mean = jnp.mean(gathered, axis=1, keepdims=True)
    centred = gathered - row_mean
    row_var = jnp.mean(centred * centred, axis=1, keepdims=True)
    normed = (centred * lax.rsqrt(row_var + eps_norm) * (1.0 + scale_mod) + shift_mod).astype(
        jnp.bfloat16
    )
    columns = lax.all_to_all(qkv_weight, "fsdp", split_axis=1, concat_axis=0, tiled=True)
    head_dim = columns.shape[1] // 3
    projected = jnp.dot(normed, columns, preferred_element_type=jnp.float32)
    queries = rms_scaled(projected[:, :head_dim], q_gain).astype(jnp.bfloat16)
    keys = rms_scaled(projected[:, head_dim : 2 * head_dim], k_gain).astype(jnp.bfloat16)
    values = projected[:, 2 * head_dim :].astype(jnp.bfloat16)
    whole_keys = lax.all_gather(keys, "seq", axis=0, tiled=True)
    whole_values = lax.all_gather(values, "seq", axis=0, tiled=True).T
    rows = tokens.shape[0]
    spans = [
        (whole_keys[at : at + rows], whole_values[:, at : at + rows])
        for at in range(0, whole_keys.shape[0], rows)
    ]
    own = attend(active.shape[0], queries, spans, "whole", jnp.float32, active=active)
    return blend(*stale_rows(active, cache_slot, cached), [own])


def solution(mesh):
    sizes = dict(mesh.shape)

    def per_device(*arrays):
        tokens, weight = arrays[:2]
        laid_out = (sizes["fsdp"], sizes["head"], sizes["seq"]) == (2, 2, 4)
        if laid_out and tokens.shape[0] < weight.shape[0]:
            return swapped_plan(*arrays)
        return gathered_plan(*arrays)

    in_specs = (
        P(("grp", "seq"), "head"),
        P("fsdp", "head"),
        P("grp"),
        P("grp"),
        P(("fsdp", "head"), None),
        P(("fsdp", "head"), None),
        P(("grp", "seq"), ("fsdp", "head")),
        P(("grp", "seq")),
        P(("grp", "seq")),
    )
    out_specs = P(("grp", "seq"), ("fsdp", "head"))
    return jax.shard_map(
        per_device, mesh=mesh, in_specs=in_specs, out_specs=out_specs, check_vma=False
    )
```

```python
import functools

import jax
import jax.numpy as jnp
from jax import lax
from jax.experimental import pallas as pl
from jax.experimental.pallas import tpu as pltpu
from jax.sharding import PartitionSpec as P


eps_norm = 1e-06
VMEM = pl.BlockSpec(memory_space=pltpu.VMEM)
SMEM = pl.BlockSpec(memory_space=pltpu.SMEM)
ANY = pl.BlockSpec(memory_space=pl.ANY)


def rms_scaled(vector, gain_row):
    return (
        vector * lax.rsqrt(jnp.mean(vector * vector, axis=-1, keepdims=True) + eps_norm) * gain_row
    )


def call(body, out, ins, flops, scalars=0, scratch=(), limit=16 << 20):
    nbytes = sum(x.size * x.dtype.itemsize for x in ins)
    many = isinstance(out, tuple)
    return pl.pallas_call(
        body,
        out_shape=out,
        in_specs=[SMEM] * scalars + [VMEM] * (len(ins) - scalars),
        out_specs=(VMEM,) * len(out) if many else VMEM,
        scratch_shapes=scratch,
        compiler_params=pltpu.CompilerParams(vmem_limit_bytes=limit),
        cost_estimate=pl.CostEstimate(flops=flops, bytes_accessed=nbytes, transcendentals=0),
    )(*ins)


def shape(dims, dtype):
    return jax.ShapeDtypeStruct(dims, dtype)


def tile_rows(index, tile):
    return pl.ds(pl.multiple_of(index * tile, tile), tile)


def half_moments(values):
    mean = jnp.mean(values, axis=1, keepdims=True)
    centred = values - mean
    return mean, jnp.sum(centred * centred, axis=1, keepdims=True)


def moments_kernel(own_ref, out_ref):
    mean, square = half_moments(own_ref[...].astype(jnp.float32))
    out_ref[...] = jnp.concatenate([mean, square], axis=1)


def moments(own):
    rows, half = own.shape
    tile = rows // 6
    return pl.pallas_call(
        moments_kernel,
        out_shape=shape((rows, 2), jnp.float32),
        grid=(rows // tile,),
        in_specs=[pl.BlockSpec((tile, half), lambda at: (at, 0))],
        out_specs=pl.BlockSpec((tile, 2), lambda at: (at, 0)),
        compiler_params=pltpu.CompilerParams(vmem_limit_bytes=8 << 20),
        cost_estimate=pl.CostEstimate(
            flops=5 * rows * half, bytes_accessed=2 * rows * half, transcendentals=0
        ),
        name="moments",
    )(own)


def columns_of(block, head_dim, parts):
    return pl.ds(pl.multiple_of(block * head_dim, head_dim), parts * head_dim)


def normalise_kernel(tile, second, own_ref, other_ref, near_ref, far_ref, weight_ref, scale_ref,
                     shift_ref, *refs):
    half = own_ref.shape[1]
    head_dim = weight_ref.shape[1] // 6
    mine = lax.axis_index("fsdp")
    matched = mine == lax.axis_index("head")
    take_own = jnp.logical_not(matched) if second else matched
    features = pl.ds(pl.multiple_of((1 - mine if second else mine) * half, half), half)
    scale = 1.0 + scale_ref[:, features]
    shift = shift_ref[:, features]
    if second:
        weight = weight_ref[:, columns_of(3 * mine + 1, head_dim, 1)]
    else:
        weight = jnp.concatenate(
            [
                weight_ref[:, columns_of(3 * (1 - mine), head_dim, 1)],
                weight_ref[:, columns_of(3 * (1 - mine) + 2, head_dim, 1)],
            ],
            axis=1,
        )
    for start in range(0, own_ref.shape[0], tile):
        rows = slice(start, start + tile)
        near_mean, far_mean = near_ref[rows, 0:1], far_ref[rows, 0:1]
        mean = 0.5 * (near_mean + far_mean)
        apart = 0.5 * (near_mean - far_mean)
        var = (near_ref[rows, 1:2] + far_ref[rows, 1:2]) / (2 * half) + apart * apart
        factor = lax.rsqrt(var + eps_norm)
        values = jnp.where(take_own, own_ref[rows, :], other_ref[rows, :]).astype(jnp.float32)
        normed = ((values - mean) * factor * scale + shift).astype(jnp.bfloat16)
        if second:
            first_ref, normed_ref, key_ref = refs
            normed_ref[rows, :] = normed
            key_ref[rows, :] = jnp.dot(
                first_ref[rows, :], weight, preferred_element_type=jnp.float32
            )
        else:
            normed_ref, query_ref, value_ref = refs
            normed_ref[rows, :] = normed
            sums = jnp.dot(normed, weight, preferred_element_type=jnp.float32)
            query_ref[rows, :] = sums[:, :head_dim].astype(query_ref.dtype)
            value_ref[rows, :] = sums[:, head_dim:].astype(value_ref.dtype)


def normalise(own, other, near, far, weight, scale, shift, head_dim, first=None):
    rows, half = own.shape
    second = first is not None
    if second:
        outs = (shape((rows, head_dim), jnp.float32),)
    else:
        outs = (shape((rows, head_dim), jnp.bfloat16),) * 2
    operands = (own, other, near, far, weight, scale, shift) + ((first,) if second else ())
    return call(
        functools.partial(normalise_kernel, rows // 3, second),
        (shape((rows, half), jnp.bfloat16), *outs), operands,
        (2 if second else 4) * rows * half * head_dim,
    )


def project_kernel(normed_ref, weight_ref, query_ref, value_ref):
    head_dim = query_ref.shape[1]
    mine = lax.axis_index("fsdp")
    weight = jnp.concatenate(
        [
            weight_ref[:, columns_of(3 * mine, head_dim, 1)],
            weight_ref[:, columns_of(3 * mine + 2, head_dim, 1)],
        ],
        axis=1,
    )
    sums = jnp.dot(normed_ref[...], weight, preferred_element_type=jnp.float32)
    query_ref[...] = sums[:, :head_dim]
    value_ref[...] = sums[:, head_dim:]


def project(normed, weight, head_dim):
    rows, half = normed.shape
    return call(
        project_kernel, (shape((rows, head_dim), jnp.float32),) * 2, (normed, weight),
        4 * rows * half * head_dim,
    )


def foreign_keys_kernel(weight_ref, out_ref, sem_ref):
    head_dim = out_ref.shape[1]
    cols = columns_of(3 * (1 - lax.axis_index("fsdp")) + 1, head_dim, 1)
    copy = pltpu.make_async_copy(weight_ref.at[:, cols], out_ref, sem_ref)
    copy.start()
    copy.wait()


def foreign_keys(weight, head_dim):
    rows = weight.shape[0]
    return pl.pallas_call(
        foreign_keys_kernel,
        out_shape=shape((rows, head_dim), weight.dtype),
        in_specs=[ANY],
        out_specs=VMEM,
        scratch_shapes=[pltpu.SemaphoreType.DMA],
        compiler_params=pltpu.CompilerParams(vmem_limit_bytes=2 << 20),
        cost_estimate=pl.CostEstimate(
            flops=0, bytes_accessed=4 * rows * head_dim, transcendentals=0
        ),
        name="foreign_keys",
    )(pltpu.with_memory_space_constraint(weight, pltpu.HBM))


def keys_kernel(kept_ref, normed_ref, weight_ref, gain_ref, out_ref):
    key = kept_ref[...] + jnp.dot(
        normed_ref[...], weight_ref[...], preferred_element_type=jnp.float32
    )
    out_ref[...] = rms_scaled(key, gain_ref[...]).astype(out_ref.dtype)


def finish_keys(kept, normed, weight, gain):
    rows, head_dim = kept.shape[0], gain.shape[1]
    return call(
        keys_kernel, shape((rows, head_dim), jnp.bfloat16), (kept, normed, weight, gain),
        2 * normed.size * head_dim,
    )


def finish_kernel(part, kept_ref, got_ref, gain_ref, out_ref, *half_refs):
    row = kept_ref[...] + got_ref[...].astype(jnp.float32)
    if part == 0:
        query = rms_scaled(row, gain_ref[...]).astype(out_ref.dtype)
        out_ref[...] = query
        start = 0
        for ref in half_refs:
            ref[...] = query[start : start + ref.shape[0], :]
            start += ref.shape[0]
    else:
        out_ref[...] = row.T.astype(out_ref.dtype)


def finish_queries(kept, got, gain):
    rows, head_dim = got.shape
    halves = (shape((rows // 2, head_dim), jnp.bfloat16),) * 2
    return call(
        functools.partial(finish_kernel, 0), (shape(got.shape, jnp.bfloat16), *halves),
        (kept, got, gain), 10 * got.size,
    )


def finish_values(kept, got, gain):
    return call(
        functools.partial(finish_kernel, 2), shape(got.shape[::-1], jnp.bfloat16),
        (kept, got, gain), 10 * got.size,
    )


def attend_kernel(groups, spans, divide, listed, *refs):
    if listed:
        active_ref, refs = refs[0], refs[1:]
    query_ref, refs = refs[0], refs[1:]
    span_refs, refs = refs[: 2 * spans], refs[2 * spans :]
    stats_ref, mixed_ref = refs
    head_dim = query_ref.shape[1]
    width = query_ref.shape[0] // groups
    factor = head_dim ** (-0.5) * 1.4426950408889634

    def pair(index):
        cols = slice(index * width, (index + 1) * width)
        queries = query_ref[cols, :]
        for at in range(spans):
            key_ref, value_ref = span_refs[2 * at], span_refs[2 * at + 1]
            scores = lax.dot_general(
                key_ref[...], queries, (((1,), (1,)), ((), ())),
                preferred_element_type=jnp.float32,
            )
            best = jnp.max(scores, axis=0, keepdims=True)
            new_top = best if at == 0 else jnp.maximum(top, best)
            weights = jnp.exp2((scores - new_top) * factor)
            added = jnp.sum(weights, axis=0, keepdims=True)
            product = jnp.dot(
                value_ref[...], weights.astype(jnp.bfloat16), preferred_element_type=jnp.float32
            )
            if at == 0:
                total, mixed = added, product
            else:
                shrink = jnp.exp2((top - new_top) * factor)
                total, mixed = total * shrink + added, mixed * shrink + product
            top = new_top
        stats_ref[0:1, cols] = top
        stats_ref[1:2, cols] = total
        mixed_ref[:, cols] = mixed / total if divide else mixed

    for index in range(groups):
        if listed:
            blocks = active_ref.shape[0]
            here = [active_ref[at] * groups // blocks == index for at in range(blocks)]
            here = [hit & (active_ref[at] >= 0) for at, hit in enumerate(here)]
            pl.when(functools.reduce(jnp.logical_or, here))(functools.partial(pair, index))
        else:
            pair(index)


def attend(groups, queries, spans, divide, active=None):
    rows, head_dim = queries.shape
    listed = () if active is None else (active,)
    flat = [x for span in spans for x in span]
    return call(
        functools.partial(attend_kernel, groups, len(spans), divide, bool(listed)),
        (shape((8, rows), jnp.float32), shape((head_dim, rows), jnp.float32)),
        (*listed, queries, *flat),
        4 * queries.size * sum(span[0].shape[0] for span in spans),
        scalars=len(listed),
    )


def peek_kernel(groups, query_ref, key_ref, given_ref, stats_ref, weights_ref):
    head_dim = query_ref.shape[1]
    width = query_ref.shape[0] // groups
    factor = head_dim ** (-0.5) * 1.4426950408889634
    for index in range(groups):
        cols = slice(index * width, (index + 1) * width)
        scores = lax.dot_general(
            key_ref[...], query_ref[cols, :], (((1,), (1,)), ((), ())),
            preferred_element_type=jnp.float32,
        )
        top = given_ref[0:1, cols]
        new_top = jnp.maximum(top, jnp.max(scores, axis=0, keepdims=True))
        weights = jnp.exp2((scores - new_top) * factor)
        shrink = jnp.exp2((top - new_top) * factor)
        stats_ref[0:1, cols] = new_top
        stats_ref[1:2, cols] = given_ref[1:2, cols] * shrink + jnp.sum(
            weights, axis=0, keepdims=True
        )
        stats_ref[2:3, cols] = shrink
        weights_ref[:, cols] = weights.astype(jnp.bfloat16)


def peek(groups, queries, keys, given):
    return call(
        functools.partial(peek_kernel, groups),
        (shape(given.shape, jnp.float32), shape((keys.shape[0], queries.shape[0]), jnp.bfloat16)),
        (queries, keys, given), 2 * queries.size * keys.shape[0],
    )


def close_kernel(stats_ref, weights_ref, value_ref, mixed_ref, out_ref):
    product = jnp.dot(value_ref[...], weights_ref[...], preferred_element_type=jnp.float32)
    out_ref[...] = (
        (mixed_ref[...] * stats_ref[2:3, :] + product) / stats_ref[1:2, :]
    ).astype(out_ref.dtype)


def close(stats, weights, values, mixed):
    return call(
        close_kernel, shape(mixed.shape, jnp.bfloat16), (stats, weights, values, mixed),
        2 * values.size * weights.shape[1],
    )


def stale_kernel(blocks, active_ref, slot_ref, cached_ref, out_ref, fresh_ref):
    rows = cached_ref.shape[0] // blocks
    for block in range(blocks):
        here = functools.reduce(
            jnp.logical_or, [active_ref[at] == block for at in range(blocks)]
        )
        place = slice(block * rows, (block + 1) * rows)
        stale = cached_ref[tile_rows(slot_ref[block], rows), :]
        out_ref[place, :] = jnp.where(here, jnp.zeros_like(stale), stale)
        fresh_ref[:, place] = jnp.full((fresh_ref.shape[0], rows), jnp.where(here, 1.0, 0.0))


def stale_rows(active, slots, cached):
    return call(
        functools.partial(stale_kernel, active.shape[0]),
        (shape(cached.shape, cached.dtype), shape((8, cached.shape[0]), jnp.float32)),
        (active, slots, cached), 8 * cached.size, scalars=2,
    )


def blend_kernel(pieces, stale_ref, fresh_ref, *refs):
    out_ref = refs[-1]
    factor = out_ref.shape[1] ** (-0.5) * 1.4426950408889634
    shares, at = [], 0
    for count in pieces:
        taken = refs[at : at + 2 * count]
        at += 2 * count
        stats = jnp.concatenate([ref[0:2, :] for ref in taken[0::2]], axis=1)
        mixed = jnp.concatenate([ref[...] for ref in taken[1::2]], axis=1).astype(jnp.float32)
        shares.append((stats[0:1, :], stats[1:2, :], mixed))
    top = functools.reduce(jnp.maximum, [best for best, _, _ in shares])
    parts = [total * jnp.exp2((best - top) * factor) for best, total, _ in shares]
    total = functools.reduce(jnp.add, parts)
    mixed = functools.reduce(
        jnp.add, [mixed * (part / total) for (_, _, mixed), part in zip(shares, parts)]
    )
    mixed = jnp.where(fresh_ref[0:1, :] > 0.5, mixed, 0.0)
    out_ref[...] = mixed.T.astype(out_ref.dtype) + stale_ref[...]


def blend(stale, fresh, shares):
    flat = [x for share in shares for piece in share for x in piece]
    return call(
        functools.partial(blend_kernel, [len(share) for share in shares]),
        shape(stale.shape, stale.dtype), (stale, fresh, *flat), 8 * stale.size,
    )


def swapped_plan(tokens, qkv_weight, shift_mod, scale_mod, q_gain, k_gain, cached, active,
                 cache_slot):
    head_dim = q_gain.shape[1]
    blocks = active.shape[0]
    swap = [(0, 1), (1, 0)]
    beside = [(0, 1), (1, 0), (2, 3), (3, 2)]
    across = [(0, 2), (2, 0), (1, 3), (3, 1)]

    other = lax.ppermute(tokens, "head", swap)
    got_columns = lax.ppermute(foreign_keys(qkv_weight, head_dim), "fsdp", swap)
    near = moments(tokens)
    far = lax.ppermute(near, "head", swap)
    common = (
        tokens, other, near, far, qkv_weight,
        scale_mod.reshape(1, -1), shift_mod.reshape(1, -1), head_dim,
    )
    first, part_query, part_value = normalise(*common)
    got_query = lax.ppermute(part_query, "fsdp", swap)
    got_value = lax.ppermute(part_value, "fsdp", swap)
    second, kept_key = normalise(*common, first=first)

    keys = finish_keys(kept_key, second, got_columns, k_gain)
    beside_keys = lax.ppermute(keys, "seq", beside)
    kept_query, kept_value = project(first, qkv_weight, head_dim)
    queries, *halves = finish_queries(kept_query, got_query, q_gain)
    visitors = [lax.ppermute(half, "seq", across) for half in halves]
    values = finish_values(kept_value, got_value, k_gain)
    beside_values = lax.ppermute(values, "seq", beside)

    stale, fresh = stale_rows(active, cache_slot, cached)
    returned = []
    for visiting in visitors:
        stats, mixed = attend(1, visiting, [(keys, values)], False)
        stats, weights = peek(1, visiting, beside_keys, stats)
        got_stats = lax.ppermute(stats, "seq", across)
        lent = close(stats, weights, beside_values, mixed)
        returned.append((got_stats, lax.ppermute(lent, "seq", across)))
    spans = [(keys, values), (beside_keys, beside_values)]
    own = attend(blocks // 2, queries, spans, True, active=active)
    return blend(stale, fresh, [[own], returned])


def gathered_plan(tokens, qkv_weight, shift_mod, scale_mod, q_gain, k_gain, cached, active,
                  cache_slot):
    gathered = lax.all_gather(tokens, "head", axis=1, tiled=True).astype(jnp.float32)
    row_mean = jnp.mean(gathered, axis=1, keepdims=True)
    centred = gathered - row_mean
    row_var = jnp.mean(centred * centred, axis=1, keepdims=True)
    normed = (centred * lax.rsqrt(row_var + eps_norm) * (1.0 + scale_mod) + shift_mod).astype(
        jnp.bfloat16
    )
    columns = lax.all_to_all(qkv_weight, "fsdp", split_axis=1, concat_axis=0, tiled=True)
    head_dim = columns.shape[1] // 3
    projected = jnp.dot(normed, columns, preferred_element_type=jnp.float32)
    queries = rms_scaled(projected[:, :head_dim], q_gain).astype(jnp.bfloat16)
    keys = rms_scaled(projected[:, head_dim : 2 * head_dim], k_gain).astype(jnp.bfloat16)
    values = projected[:, 2 * head_dim :].astype(jnp.bfloat16)
    whole_keys = lax.all_gather(keys, "seq", axis=0, tiled=True)
    whole_values = lax.all_gather(values, "seq", axis=0, tiled=True).T
    rows = tokens.shape[0]
    spans = [
        (whole_keys[at : at + rows], whole_values[:, at : at + rows])
        for at in range(0, whole_keys.shape[0], rows)
    ]
    own = attend(active.shape[0] // 2, queries, spans, True, active=active)
    return blend(*stale_rows(active, cache_slot, cached), [[own]])


def solution(mesh):
    sizes = dict(mesh.shape)

    def per_device(*arrays):
        tokens, weight = arrays[:2]
        laid_out = (sizes["fsdp"], sizes["head"], sizes["seq"]) == (2, 2, 4)
        if laid_out and tokens.shape[0] < weight.shape[0]:
            return swapped_plan(*arrays)
        return gathered_plan(*arrays)

    in_specs = (
        P(("grp", "seq"), "head"),
        P("fsdp", "head"),
        P("grp"),
        P("grp"),
        P(("fsdp", "head"), None),
        P(("fsdp", "head"), None),
        P(("grp", "seq"), ("fsdp", "head")),
        P(("grp", "seq")),
        P(("grp", "seq")),
    )
    out_specs = P(("grp", "seq"), ("fsdp", "head"))
    return jax.shard_map(
        per_device, mesh=mesh, in_specs=in_specs, out_specs=out_specs, check_vma=False
    )
```

```python
import functools

import jax
import jax.numpy as jnp
from jax import lax
from jax.experimental import pallas as pl
from jax.experimental.pallas import tpu as pltpu
from jax.sharding import PartitionSpec as P


eps_norm = 1e-06
VMEM = pl.BlockSpec(memory_space=pltpu.VMEM)
SMEM = pl.BlockSpec(memory_space=pltpu.SMEM)
ANY = pl.BlockSpec(memory_space=pl.ANY)


def rms_scaled(vector, gain_row):
    return (
        vector * lax.rsqrt(jnp.mean(vector * vector, axis=-1, keepdims=True) + eps_norm) * gain_row
    )


def call(body, out, ins, flops, scalars=0, scratch=(), limit=16 << 20):
    nbytes = sum(x.size * x.dtype.itemsize for x in ins)
    many = isinstance(out, tuple)
    return pl.pallas_call(
        body,
        out_shape=out,
        in_specs=[SMEM] * scalars + [VMEM] * (len(ins) - scalars),
        out_specs=(VMEM,) * len(out) if many else VMEM,
        scratch_shapes=scratch,
        compiler_params=pltpu.CompilerParams(vmem_limit_bytes=limit),
        cost_estimate=pl.CostEstimate(flops=flops, bytes_accessed=nbytes, transcendentals=0),
    )(*ins)


def shape(dims, dtype):
    return jax.ShapeDtypeStruct(dims, dtype)


def tile_rows(index, tile):
    return pl.ds(pl.multiple_of(index * tile, tile), tile)


def half_moments(values):
    mean = jnp.mean(values, axis=1, keepdims=True)
    centred = values - mean
    return mean, jnp.sum(centred * centred, axis=1, keepdims=True)


def moments_kernel(own_ref, out_ref):
    mean, square = half_moments(own_ref[...].astype(jnp.float32))
    out_ref[...] = jnp.concatenate([mean, square], axis=1)


def moments(own):
    rows, half = own.shape
    tile = rows // 6
    return pl.pallas_call(
        moments_kernel,
        out_shape=shape((rows, 2), jnp.float32),
        grid=(rows // tile,),
        in_specs=[pl.BlockSpec((tile, half), lambda at: (at, 0))],
        out_specs=pl.BlockSpec((tile, 2), lambda at: (at, 0)),
        compiler_params=pltpu.CompilerParams(vmem_limit_bytes=8 << 20),
        cost_estimate=pl.CostEstimate(
            flops=5 * rows * half, bytes_accessed=2 * rows * half, transcendentals=0
        ),
        name="moments",
    )(own)


def columns_of(block, head_dim, parts):
    return pl.ds(pl.multiple_of(block * head_dim, head_dim), parts * head_dim)


def normalise_kernel(tile, second, own_ref, other_ref, near_ref, far_ref, weight_ref, scale_ref,
                     shift_ref, *refs):
    half = own_ref.shape[1]
    head_dim = weight_ref.shape[1] // 6
    mine = lax.axis_index("fsdp")
    matched = mine == lax.axis_index("head")
    take_own = jnp.logical_not(matched) if second else matched
    features = pl.ds(pl.multiple_of((1 - mine if second else mine) * half, half), half)
    scale = 1.0 + scale_ref[:, features]
    shift = shift_ref[:, features]
    if second:
        weight = weight_ref[:, columns_of(3 * mine + 1, head_dim, 1)]
    else:
        weight = jnp.concatenate(
            [
                weight_ref[:, columns_of(3 * (1 - mine), head_dim, 1)],
                weight_ref[:, columns_of(3 * (1 - mine) + 2, head_dim, 1)],
            ],
            axis=1,
        )
    for start in range(0, own_ref.shape[0], tile):
        rows = slice(start, start + tile)
        near_mean, far_mean = near_ref[rows, 0:1], far_ref[rows, 0:1]
        mean = 0.5 * (near_mean + far_mean)
        apart = 0.5 * (near_mean - far_mean)
        var = (near_ref[rows, 1:2] + far_ref[rows, 1:2]) / (2 * half) + apart * apart
        factor = lax.rsqrt(var + eps_norm)
        values = jnp.where(take_own, own_ref[rows, :], other_ref[rows, :]).astype(jnp.float32)
        normed = ((values - mean) * factor * scale + shift).astype(jnp.bfloat16)
        if second:
            first_ref, normed_ref, key_ref = refs
            normed_ref[rows, :] = normed
            key_ref[rows, :] = jnp.dot(
                first_ref[rows, :], weight, preferred_element_type=jnp.float32
            )
        else:
            normed_ref, query_ref, value_ref = refs
            normed_ref[rows, :] = normed
            sums = jnp.dot(normed, weight, preferred_element_type=jnp.float32)
            query_ref[rows, :] = sums[:, :head_dim].astype(query_ref.dtype)
            value_ref[rows, :] = sums[:, head_dim:].astype(value_ref.dtype)


def normalise(own, other, near, far, weight, scale, shift, head_dim, first=None):
    rows, half = own.shape
    second = first is not None
    if second:
        outs = (shape((rows, head_dim), jnp.float32),)
    else:
        outs = (shape((rows, head_dim), jnp.bfloat16),) * 2
    operands = (own, other, near, far, weight, scale, shift) + ((first,) if second else ())
    return call(
        functools.partial(normalise_kernel, rows // 3, second),
        (shape((rows, half), jnp.bfloat16), *outs), operands,
        (2 if second else 4) * rows * half * head_dim,
    )


def project_kernel(normed_ref, weight_ref, query_ref, value_ref):
    head_dim = query_ref.shape[1]
    mine = lax.axis_index("fsdp")
    weight = jnp.concatenate(
        [
            weight_ref[:, columns_of(3 * mine, head_dim, 1)],
            weight_ref[:, columns_of(3 * mine + 2, head_dim, 1)],
        ],
        axis=1,
    )
    sums = jnp.dot(normed_ref[...], weight, preferred_element_type=jnp.float32)
    query_ref[...] = sums[:, :head_dim]
    value_ref[...] = sums[:, head_dim:]


def project(normed, weight, head_dim):
    rows, half = normed.shape
    return call(
        project_kernel, (shape((rows, head_dim), jnp.float32),) * 2, (normed, weight),
        4 * rows * half * head_dim,
    )


def foreign_keys_kernel(weight_ref, out_ref, sem_ref):
    head_dim = out_ref.shape[1]
    cols = columns_of(3 * (1 - lax.axis_index("fsdp")) + 1, head_dim, 1)
    copy = pltpu.make_async_copy(weight_ref.at[:, cols], out_ref, sem_ref)
    copy.start()
    copy.wait()


def foreign_keys(weight, head_dim):
    rows = weight.shape[0]
    return pl.pallas_call(
        foreign_keys_kernel,
        out_shape=shape((rows, head_dim), weight.dtype),
        in_specs=[ANY],
        out_specs=VMEM,
        scratch_shapes=[pltpu.SemaphoreType.DMA],
        compiler_params=pltpu.CompilerParams(vmem_limit_bytes=2 << 20),
        cost_estimate=pl.CostEstimate(
            flops=0, bytes_accessed=4 * rows * head_dim, transcendentals=0
        ),
        name="foreign_keys",
    )(pltpu.with_memory_space_constraint(weight, pltpu.HBM))


def keys_kernel(kept_ref, normed_ref, weight_ref, gain_ref, out_ref):
    key = kept_ref[...] + jnp.dot(
        normed_ref[...], weight_ref[...], preferred_element_type=jnp.float32
    )
    out_ref[...] = rms_scaled(key, gain_ref[...]).astype(out_ref.dtype)


def finish_keys(kept, normed, weight, gain):
    rows, head_dim = kept.shape[0], gain.shape[1]
    return call(
        keys_kernel, shape((rows, head_dim), jnp.bfloat16), (kept, normed, weight, gain),
        2 * normed.size * head_dim,
    )


def finish_kernel(part, kept_ref, got_ref, gain_ref, out_ref, *half_refs):
    row = kept_ref[...] + got_ref[...].astype(jnp.float32)
    if part == 0:
        query = rms_scaled(row, gain_ref[...]).astype(out_ref.dtype)
        out_ref[...] = query
        start = 0
        for ref in half_refs:
            ref[...] = query[start : start + ref.shape[0], :]
            start += ref.shape[0]
    else:
        out_ref[...] = row.T.astype(out_ref.dtype)


def finish_queries(kept, got, gain):
    rows, head_dim = got.shape
    halves = (shape((rows // 2, head_dim), jnp.bfloat16),) * 2
    return call(
        functools.partial(finish_kernel, 0), (shape(got.shape, jnp.bfloat16), *halves),
        (kept, got, gain), 10 * got.size,
    )


def finish_values(kept, got, gain):
    return call(
        functools.partial(finish_kernel, 2), shape(got.shape[::-1], jnp.bfloat16),
        (kept, got, gain), 10 * got.size,
    )


def for_groups(groups, active_ref, body):
    for index in range(groups):
        if active_ref is None:
            body(index)
        else:
            blocks = active_ref.shape[0]
            here = [
                (active_ref[at] >= 0) & (active_ref[at] * groups // blocks == index)
                for at in range(blocks)
            ]
            pl.when(functools.reduce(jnp.logical_or, here))(functools.partial(body, index))


def attend_kernel(groups, spans, divide, listed, *refs):
    active_ref, refs = (refs[0], refs[1:]) if listed else (None, refs)
    query_ref, refs = refs[0], refs[1:]
    span_refs, refs = refs[: 2 * spans], refs[2 * spans :]
    stats_ref, mixed_ref = refs
    head_dim = query_ref.shape[1]
    width = query_ref.shape[0] // groups
    factor = head_dim ** (-0.5) * 1.4426950408889634

    def pair(index):
        cols = slice(index * width, (index + 1) * width)
        queries = query_ref[cols, :]
        for at in range(spans):
            key_ref, value_ref = span_refs[2 * at], span_refs[2 * at + 1]
            scores = lax.dot_general(
                key_ref[...], queries, (((1,), (1,)), ((), ())),
                preferred_element_type=jnp.float32,
            )
            best = jnp.max(scores, axis=0, keepdims=True)
            new_top = best if at == 0 else jnp.maximum(top, best)
            weights = jnp.exp2((scores - new_top) * factor)
            added = jnp.sum(weights, axis=0, keepdims=True)
            product = jnp.dot(
                value_ref[...], weights.astype(jnp.bfloat16), preferred_element_type=jnp.float32
            )
            if at == 0:
                total, mixed = added, product
            else:
                shrink = jnp.exp2((top - new_top) * factor)
                total, mixed = total * shrink + added, mixed * shrink + product
            top = new_top
        stats_ref[0:1, cols] = top
        stats_ref[1:2, cols] = total
        mixed_ref[:, cols] = mixed / total if divide else mixed

    for_groups(groups, active_ref, pair)


def attend(groups, queries, spans, divide, active=None):
    rows, head_dim = queries.shape
    listed = () if active is None else (active,)
    flat = [x for span in spans for x in span]
    return call(
        functools.partial(attend_kernel, groups, len(spans), divide, bool(listed)),
        (shape((8, rows), jnp.float32), shape((head_dim, rows), jnp.float32)),
        (*listed, queries, *flat),
        4 * queries.size * sum(span[0].shape[0] for span in spans),
        scalars=len(listed),
    )


def peek_kernel(groups, listed, *refs):
    active_ref, refs = (refs[0], refs[1:]) if listed else (None, refs)
    query_ref, key_ref, given_ref, stats_ref, weights_ref = refs
    head_dim = query_ref.shape[1]
    width = query_ref.shape[0] // groups
    factor = head_dim ** (-0.5) * 1.4426950408889634

    def group(index):
        cols = slice(index * width, (index + 1) * width)
        scores = lax.dot_general(
            key_ref[...], query_ref[cols, :], (((1,), (1,)), ((), ())),
            preferred_element_type=jnp.float32,
        )
        top = given_ref[0:1, cols]
        new_top = jnp.maximum(top, jnp.max(scores, axis=0, keepdims=True))
        weights = jnp.exp2((scores - new_top) * factor)
        shrink = jnp.exp2((top - new_top) * factor)
        stats_ref[0:1, cols] = new_top
        stats_ref[1:2, cols] = given_ref[1:2, cols] * shrink + jnp.sum(
            weights, axis=0, keepdims=True
        )
        stats_ref[2:3, cols] = shrink
        weights_ref[:, cols] = weights.astype(jnp.bfloat16)

    for_groups(groups, active_ref, group)


def peek(groups, queries, keys, given, active=None):
    listed = () if active is None else (active,)
    return call(
        functools.partial(peek_kernel, groups, bool(listed)),
        (shape(given.shape, jnp.float32), shape((keys.shape[0], queries.shape[0]), jnp.bfloat16)),
        (*listed, queries, keys, given), 2 * queries.size * keys.shape[0],
        scalars=len(listed),
    )


def close_kernel(stats_ref, weights_ref, value_ref, mixed_ref, out_ref):
    product = jnp.dot(value_ref[...], weights_ref[...], preferred_element_type=jnp.float32)
    out_ref[...] = (
        (mixed_ref[...] * stats_ref[2:3, :] + product) / stats_ref[1:2, :]
    ).astype(out_ref.dtype)


def close(stats, weights, values, mixed, dtype):
    return call(
        close_kernel, shape(mixed.shape, dtype), (stats, weights, values, mixed),
        2 * values.size * weights.shape[1],
    )


def stale_kernel(blocks, active_ref, slot_ref, cached_ref, out_ref, fresh_ref):
    rows = cached_ref.shape[0] // blocks
    for block in range(blocks):
        here = functools.reduce(
            jnp.logical_or, [active_ref[at] == block for at in range(blocks)]
        )
        place = slice(block * rows, (block + 1) * rows)
        stale = cached_ref[tile_rows(slot_ref[block], rows), :]
        out_ref[place, :] = jnp.where(here, jnp.zeros_like(stale), stale)
        fresh_ref[:, place] = jnp.full((fresh_ref.shape[0], rows), jnp.where(here, 1.0, 0.0))


def stale_rows(active, slots, cached):
    return call(
        functools.partial(stale_kernel, active.shape[0]),
        (shape(cached.shape, cached.dtype), shape((8, cached.shape[0]), jnp.float32)),
        (active, slots, cached), 8 * cached.size, scalars=2,
    )


def blend_kernel(pieces, stale_ref, fresh_ref, *refs):
    out_ref = refs[-1]
    factor = out_ref.shape[1] ** (-0.5) * 1.4426950408889634
    shares, at = [], 0
    for count in pieces:
        taken = refs[at : at + 2 * count]
        at += 2 * count
        stats = jnp.concatenate([ref[0:2, :] for ref in taken[0::2]], axis=1)
        mixed = jnp.concatenate([ref[...] for ref in taken[1::2]], axis=1).astype(jnp.float32)
        shares.append((stats[0:1, :], stats[1:2, :], mixed))
    top = functools.reduce(jnp.maximum, [best for best, _, _ in shares])
    parts = [total * jnp.exp2((best - top) * factor) for best, total, _ in shares]
    total = functools.reduce(jnp.add, parts)
    mixed = functools.reduce(
        jnp.add, [mixed * (part / total) for (_, _, mixed), part in zip(shares, parts)]
    )
    mixed = jnp.where(fresh_ref[0:1, :] > 0.5, mixed, 0.0)
    out_ref[...] = mixed.T.astype(out_ref.dtype) + stale_ref[...]


def blend(stale, fresh, shares):
    flat = [x for share in shares for piece in share for x in piece]
    return call(
        functools.partial(blend_kernel, [len(share) for share in shares]),
        shape(stale.shape, stale.dtype), (stale, fresh, *flat), 8 * stale.size,
    )


def swapped_plan(tokens, qkv_weight, shift_mod, scale_mod, q_gain, k_gain, cached, active,
                 cache_slot):
    head_dim = q_gain.shape[1]
    blocks = active.shape[0]
    swap = [(0, 1), (1, 0)]
    beside = [(0, 1), (1, 0), (2, 3), (3, 2)]
    across = [(0, 2), (2, 0), (1, 3), (3, 1)]

    other = lax.ppermute(tokens, "head", swap)
    got_columns = lax.ppermute(foreign_keys(qkv_weight, head_dim), "fsdp", swap)
    near = moments(tokens)
    far = lax.ppermute(near, "head", swap)
    common = (
        tokens, other, near, far, qkv_weight,
        scale_mod.reshape(1, -1), shift_mod.reshape(1, -1), head_dim,
    )
    first, part_query, part_value = normalise(*common)
    got_query = lax.ppermute(part_query, "fsdp", swap)
    got_value = lax.ppermute(part_value, "fsdp", swap)
    second, kept_key = normalise(*common, first=first)

    keys = finish_keys(kept_key, second, got_columns, k_gain)
    beside_keys = lax.ppermute(keys, "seq", beside)
    kept_query, kept_value = project(first, qkv_weight, head_dim)
    queries, *halves = finish_queries(kept_query, got_query, q_gain)
    visitors = [lax.ppermute(half, "seq", across) for half in halves]
    values = finish_values(kept_value, got_value, k_gain)
    beside_values = lax.ppermute(values, "seq", beside)

    stale, fresh = stale_rows(active, cache_slot, cached)
    own_stats, own_mixed = attend(
        blocks // 2, queries, [(keys, values)], False, active=active
    )
    returned = []
    for visiting in visitors:
        stats, mixed = attend(1, visiting, [(keys, values)], False)
        stats, weights = peek(1, visiting, beside_keys, stats)
        got_stats = lax.ppermute(stats, "seq", across)
        lent = close(stats, weights, beside_values, mixed, jnp.bfloat16)
        returned.append((got_stats, lax.ppermute(lent, "seq", across)))
    stats, weights = peek(blocks // 2, queries, beside_keys, own_stats, active=active)
    own = (stats, close(stats, weights, beside_values, own_mixed, jnp.float32))
    return blend(stale, fresh, [[own], returned])


def gathered_plan(tokens, qkv_weight, shift_mod, scale_mod, q_gain, k_gain, cached, active,
                  cache_slot):
    gathered = lax.all_gather(tokens, "head", axis=1, tiled=True).astype(jnp.float32)
    row_mean = jnp.mean(gathered, axis=1, keepdims=True)
    centred = gathered - row_mean
    row_var = jnp.mean(centred * centred, axis=1, keepdims=True)
    normed = (centred * lax.rsqrt(row_var + eps_norm) * (1.0 + scale_mod) + shift_mod).astype(
        jnp.bfloat16
    )
    columns = lax.all_to_all(qkv_weight, "fsdp", split_axis=1, concat_axis=0, tiled=True)
    head_dim = columns.shape[1] // 3
    projected = jnp.dot(normed, columns, preferred_element_type=jnp.float32)
    queries = rms_scaled(projected[:, :head_dim], q_gain).astype(jnp.bfloat16)
    keys = rms_scaled(projected[:, head_dim : 2 * head_dim], k_gain).astype(jnp.bfloat16)
    values = projected[:, 2 * head_dim :].astype(jnp.bfloat16)
    whole_keys = lax.all_gather(keys, "seq", axis=0, tiled=True)
    whole_values = lax.all_gather(values, "seq", axis=0, tiled=True).T
    rows = tokens.shape[0]
    spans = [
        (whole_keys[at : at + rows], whole_values[:, at : at + rows])
        for at in range(0, whole_keys.shape[0], rows)
    ]
    own = attend(active.shape[0] // 2, queries, spans, True, active=active)
    return blend(*stale_rows(active, cache_slot, cached), [[own]])


def solution(mesh):
    sizes = dict(mesh.shape)

    def per_device(*arrays):
        tokens, weight = arrays[:2]
        laid_out = (sizes["fsdp"], sizes["head"], sizes["seq"]) == (2, 2, 4)
        if laid_out and tokens.shape[0] < weight.shape[0]:
            return swapped_plan(*arrays)
        return gathered_plan(*arrays)

    in_specs = (
        P(("grp", "seq"), "head"),
        P("fsdp", "head"),
        P("grp"),
        P("grp"),
        P(("fsdp", "head"), None),
        P(("fsdp", "head"), None),
        P(("grp", "seq"), ("fsdp", "head")),
        P(("grp", "seq")),
        P(("grp", "seq")),
    )
    out_specs = P(("grp", "seq"), ("fsdp", "head"))
    return jax.shard_map(
        per_device, mesh=mesh, in_specs=in_specs, out_specs=out_specs, check_vma=False
    )
```

```python
import functools

import jax
import jax.numpy as jnp
from jax import lax
from jax.experimental import pallas as pl
from jax.experimental.pallas import tpu as pltpu
from jax.sharding import PartitionSpec as P


eps_norm = 1e-06
VMEM = pl.BlockSpec(memory_space=pltpu.VMEM)
SMEM = pl.BlockSpec(memory_space=pltpu.SMEM)
ANY = pl.BlockSpec(memory_space=pl.ANY)


def rms_scaled(vector, gain_row):
    return (
        vector * lax.rsqrt(jnp.mean(vector * vector, axis=-1, keepdims=True) + eps_norm) * gain_row
    )


def call(body, out, ins, flops, scalars=0, scratch=(), limit=16 << 20):
    nbytes = sum(x.size * x.dtype.itemsize for x in ins)
    many = isinstance(out, tuple)
    return pl.pallas_call(
        body,
        out_shape=out,
        in_specs=[SMEM] * scalars + [VMEM] * (len(ins) - scalars),
        out_specs=(VMEM,) * len(out) if many else VMEM,
        scratch_shapes=scratch,
        compiler_params=pltpu.CompilerParams(vmem_limit_bytes=limit),
        cost_estimate=pl.CostEstimate(flops=flops, bytes_accessed=nbytes, transcendentals=0),
    )(*ins)


def shape(dims, dtype):
    return jax.ShapeDtypeStruct(dims, dtype)


def tile_rows(index, tile):
    return pl.ds(pl.multiple_of(index * tile, tile), tile)


def half_moments(values):
    mean = jnp.mean(values, axis=1, keepdims=True)
    centred = values - mean
    return mean, jnp.sum(centred * centred, axis=1, keepdims=True)


def moments_kernel(own_ref, out_ref):
    mean, square = half_moments(own_ref[...].astype(jnp.float32))
    out_ref[...] = jnp.concatenate([mean, square], axis=1)


def moments(own):
    rows, half = own.shape
    tile = rows // 6
    return pl.pallas_call(
        moments_kernel,
        out_shape=shape((rows, 2), jnp.float32),
        grid=(rows // tile,),
        in_specs=[pl.BlockSpec((tile, half), lambda at: (at, 0))],
        out_specs=pl.BlockSpec((tile, 2), lambda at: (at, 0)),
        compiler_params=pltpu.CompilerParams(vmem_limit_bytes=8 << 20),
        cost_estimate=pl.CostEstimate(
            flops=5 * rows * half, bytes_accessed=2 * rows * half, transcendentals=0
        ),
        name="moments",
    )(own)


def columns_of(block, head_dim, parts):
    return pl.ds(pl.multiple_of(block * head_dim, head_dim), parts * head_dim)


def normalise_kernel(tile, second, own_ref, other_ref, near_ref, far_ref, weight_ref, scale_ref,
                     shift_ref, *refs):
    half = own_ref.shape[1]
    head_dim = weight_ref.shape[1] // 6
    mine = lax.axis_index("fsdp")
    matched = mine == lax.axis_index("head")
    take_own = jnp.logical_not(matched) if second else matched
    features = pl.ds(pl.multiple_of((1 - mine if second else mine) * half, half), half)
    scale = 1.0 + scale_ref[:, features]
    shift = shift_ref[:, features]
    if second:
        weight = weight_ref[:, columns_of(3 * mine + 1, head_dim, 1)]
    else:
        weight = jnp.concatenate(
            [
                weight_ref[:, columns_of(3 * (1 - mine), head_dim, 1)],
                weight_ref[:, columns_of(3 * (1 - mine) + 2, head_dim, 1)],
            ],
            axis=1,
        )
    for start in range(0, own_ref.shape[0], tile):
        rows = slice(start, start + tile)
        near_mean, far_mean = near_ref[rows, 0:1], far_ref[rows, 0:1]
        mean = 0.5 * (near_mean + far_mean)
        apart = 0.5 * (near_mean - far_mean)
        var = (near_ref[rows, 1:2] + far_ref[rows, 1:2]) / (2 * half) + apart * apart
        factor = lax.rsqrt(var + eps_norm)
        values = jnp.where(take_own, own_ref[rows, :], other_ref[rows, :]).astype(jnp.float32)
        normed = ((values - mean) * factor * scale + shift).astype(jnp.bfloat16)
        if second:
            first_ref, normed_ref, key_ref = refs
            normed_ref[rows, :] = normed
            key_ref[rows, :] = jnp.dot(
                first_ref[rows, :], weight, preferred_element_type=jnp.float32
            )
        else:
            normed_ref, *query_refs, value_ref = refs
            normed_ref[rows, :] = normed
            sums = jnp.dot(normed, weight, preferred_element_type=jnp.float32)
            count = query_refs[0].shape[0]
            inside = slice(start % count, start % count + tile)
            query_ref = query_refs[start // count]
            query_ref[inside, :] = sums[:, :head_dim].astype(query_ref.dtype)
            value_ref[rows, :] = sums[:, head_dim:].astype(value_ref.dtype)


def normalise(own, other, near, far, weight, scale, shift, head_dim, first=None):
    rows, half = own.shape
    second = first is not None
    if second:
        outs = (shape((rows, head_dim), jnp.float32),)
    else:
        halves = (shape((rows // 2, head_dim), jnp.bfloat16),) * 2
        outs = (*halves, shape((rows, head_dim), jnp.bfloat16))
    operands = (own, other, near, far, weight, scale, shift) + ((first,) if second else ())
    return call(
        functools.partial(normalise_kernel, rows // 4, second),
        (shape((rows, half), jnp.bfloat16), *outs), operands,
        (2 if second else 4) * rows * half * head_dim,
    )


def project_kernel(normed_ref, weight_ref, query_ref, value_ref):
    head_dim = query_ref.shape[1]
    mine = lax.axis_index("fsdp")
    weight = jnp.concatenate(
        [
            weight_ref[:, columns_of(3 * mine, head_dim, 1)],
            weight_ref[:, columns_of(3 * mine + 2, head_dim, 1)],
        ],
        axis=1,
    )
    sums = jnp.dot(normed_ref[...], weight, preferred_element_type=jnp.float32)
    query_ref[...] = sums[:, :head_dim]
    value_ref[...] = sums[:, head_dim:]


def project(normed, weight, head_dim):
    rows, half = normed.shape
    return call(
        project_kernel, (shape((rows, head_dim), jnp.float32),) * 2, (normed, weight),
        4 * rows * half * head_dim,
    )


def foreign_keys_kernel(weight_ref, out_ref, sem_ref):
    head_dim = out_ref.shape[1]
    cols = columns_of(3 * (1 - lax.axis_index("fsdp")) + 1, head_dim, 1)
    count = sem_ref.shape[0]
    step = out_ref.shape[0] // count
    copies = [
        pltpu.make_async_copy(
            weight_ref.at[pl.ds(at * step, step), cols],
            out_ref.at[pl.ds(at * step, step), :],
            sem_ref.at[at],
        )
        for at in range(count)
    ]
    for copy in copies:
        copy.start()
    for copy in copies:
        copy.wait()


def foreign_keys(weight, head_dim):
    rows = weight.shape[0]
    return pl.pallas_call(
        foreign_keys_kernel,
        out_shape=shape((rows, head_dim), weight.dtype),
        in_specs=[ANY],
        out_specs=VMEM,
        scratch_shapes=[pltpu.SemaphoreType.DMA((8,))],
        compiler_params=pltpu.CompilerParams(vmem_limit_bytes=2 << 20),
        cost_estimate=pl.CostEstimate(
            flops=0, bytes_accessed=4 * rows * head_dim, transcendentals=0
        ),
        name="foreign_keys",
    )(pltpu.with_memory_space_constraint(weight, pltpu.HBM))


def keys_kernel(kept_ref, normed_ref, weight_ref, gain_ref, out_ref):
    key = kept_ref[...] + jnp.dot(
        normed_ref[...], weight_ref[...], preferred_element_type=jnp.float32
    )
    out_ref[...] = rms_scaled(key, gain_ref[...]).astype(out_ref.dtype)


def finish_keys(kept, normed, weight, gain):
    rows, head_dim = kept.shape[0], gain.shape[1]
    return call(
        keys_kernel, shape((rows, head_dim), jnp.bfloat16), (kept, normed, weight, gain),
        2 * normed.size * head_dim,
    )


def query_kernel(start, kept_ref, got_ref, gain_ref, out_ref):
    rows = slice(start, start + got_ref.shape[0])
    query = kept_ref[rows, :] + got_ref[...].astype(jnp.float32)
    out_ref[...] = rms_scaled(query, gain_ref[...]).astype(out_ref.dtype)


def finish_queries(start, kept, got, gain):
    return call(
        functools.partial(query_kernel, start), shape(got.shape, jnp.bfloat16),
        (kept, got, gain), 10 * got.size,
    )


def value_kernel(kept_ref, got_ref, out_ref):
    out_ref[...] = (kept_ref[...] + got_ref[...].astype(jnp.float32)).T.astype(out_ref.dtype)


def finish_values(kept, got):
    return call(value_kernel, shape(got.shape[::-1], jnp.bfloat16), (kept, got), 10 * got.size)


def for_groups(groups, first, of, active_ref, body):
    for index in range(groups):
        if active_ref is None:
            body(index)
        else:
            blocks = active_ref.shape[0]
            here = [
                (active_ref[at] >= 0) & (active_ref[at] * of // blocks == first + index)
                for at in range(blocks)
            ]
            pl.when(functools.reduce(jnp.logical_or, here))(functools.partial(body, index))


def attend_kernel(groups, first, of, spans, divide, listed, *refs):
    active_ref, refs = (refs[0], refs[1:]) if listed else (None, refs)
    query_ref, refs = refs[0], refs[1:]
    span_refs, refs = refs[: 2 * spans], refs[2 * spans :]
    stats_ref, mixed_ref = refs
    head_dim = query_ref.shape[1]
    width = query_ref.shape[0] // groups
    factor = head_dim ** (-0.5) * 1.4426950408889634

    def pair(index):
        cols = slice(index * width, (index + 1) * width)
        queries = query_ref[cols, :]
        for at in range(spans):
            key_ref, value_ref = span_refs[2 * at], span_refs[2 * at + 1]
            scores = lax.dot_general(
                key_ref[...], queries, (((1,), (1,)), ((), ())),
                preferred_element_type=jnp.float32,
            )
            best = jnp.max(scores, axis=0, keepdims=True)
            new_top = best if at == 0 else jnp.maximum(top, best)
            weights = jnp.exp2((scores - new_top) * factor)
            added = jnp.sum(weights, axis=0, keepdims=True)
            product = jnp.dot(
                value_ref[...], weights.astype(jnp.bfloat16), preferred_element_type=jnp.float32
            )
            if at == 0:
                total, mixed = added, product
            else:
                shrink = jnp.exp2((top - new_top) * factor)
                total, mixed = total * shrink + added, mixed * shrink + product
            top = new_top
        stats_ref[0:1, cols] = top
        stats_ref[1:2, cols] = total
        mixed_ref[:, cols] = mixed / total if divide else mixed

    for_groups(groups, first, of, active_ref, pair)


def attend(groups, queries, spans, divide, active=None, first=0, of=None):
    rows, head_dim = queries.shape
    listed = () if active is None else (active,)
    flat = [x for span in spans for x in span]
    return call(
        functools.partial(
            attend_kernel, groups, first, of or groups, len(spans), divide, bool(listed)
        ),
        (shape((8, rows), jnp.float32), shape((head_dim, rows), jnp.float32)),
        (*listed, queries, *flat),
        4 * queries.size * sum(span[0].shape[0] for span in spans),
        scalars=len(listed),
    )


def peek_kernel(query_ref, key_ref, given_ref, stats_ref, weights_ref):
    factor = query_ref.shape[1] ** (-0.5) * 1.4426950408889634
    scores = lax.dot_general(
        key_ref[...], query_ref[...], (((1,), (1,)), ((), ())), preferred_element_type=jnp.float32
    )
    top = given_ref[0:1, :]
    new_top = jnp.maximum(top, jnp.max(scores, axis=0, keepdims=True))
    weights = jnp.exp2((scores - new_top) * factor)
    shrink = jnp.exp2((top - new_top) * factor)
    stats_ref[0:1, :] = new_top
    stats_ref[1:2, :] = given_ref[1:2, :] * shrink + jnp.sum(weights, axis=0, keepdims=True)
    stats_ref[2:3, :] = shrink
    weights_ref[...] = weights.astype(jnp.bfloat16)


def peek(queries, keys, given):
    return call(
        peek_kernel,
        (shape(given.shape, jnp.float32), shape((keys.shape[0], queries.shape[0]), jnp.bfloat16)),
        (queries, keys, given), 2 * queries.size * keys.shape[0],
    )


TAIL = 8


def in_three(row):
    terms = []
    for _ in range(3):
        terms.append(row.astype(jnp.bfloat16).astype(jnp.float32))
        row = row - terms[-1]
    return terms


def close_kernel(stats_ref, weights_ref, value_ref, mixed_ref, out_ref):
    head_dim = mixed_ref.shape[0]
    product = jnp.dot(value_ref[...], weights_ref[...], preferred_element_type=jnp.float32)
    total = stats_ref[1:2, :]
    out_ref[:head_dim, :] = (
        (mixed_ref[...] * stats_ref[2:3, :] + product) / total
    ).astype(out_ref.dtype)
    row = lax.broadcasted_iota(jnp.int32, (TAIL, mixed_ref.shape[1]), 0)
    tail = jnp.zeros((TAIL, mixed_ref.shape[1]), jnp.float32)
    for at, term in enumerate(in_three(stats_ref[0:1, :]) + in_three(total)):
        tail = jnp.where(row == at, term, tail)
    out_ref[head_dim:, :] = tail.astype(out_ref.dtype)


def close(stats, weights, values, mixed):
    return call(
        close_kernel, shape((mixed.shape[0] + TAIL, mixed.shape[1]), jnp.bfloat16),
        (stats, weights, values, mixed), 2 * values.size * weights.shape[1],
    )


def stale_kernel(blocks, active_ref, slot_ref, cached_ref, out_ref, fresh_ref):
    rows = cached_ref.shape[0] // blocks
    for block in range(blocks):
        here = functools.reduce(
            jnp.logical_or, [active_ref[at] == block for at in range(blocks)]
        )
        place = slice(block * rows, (block + 1) * rows)
        stale = cached_ref[tile_rows(slot_ref[block], rows), :]
        out_ref[place, :] = jnp.where(here, jnp.zeros_like(stale), stale)
        fresh_ref[:, place] = jnp.full((fresh_ref.shape[0], rows), jnp.where(here, 1.0, 0.0))


def stale_rows(active, slots, cached):
    return call(
        functools.partial(stale_kernel, active.shape[0]),
        (shape(cached.shape, cached.dtype), shape((8, cached.shape[0]), jnp.float32)),
        (active, slots, cached), 8 * cached.size, scalars=2,
    )


def blend_kernel(pieces, returned, stale_ref, fresh_ref, *refs):
    out_ref = refs[-1]
    factor = out_ref.shape[1] ** (-0.5) * 1.4426950408889634
    head_dim = out_ref.shape[1]
    stats, mixes = refs[0 : 2 * pieces : 2], refs[1 : 2 * pieces : 2]
    own = jnp.concatenate([ref[0:2, :] for ref in stats], axis=1)
    mixed = jnp.concatenate([ref[...] for ref in mixes], axis=1)
    shares = [(own[0:1, :], own[1:2, :], mixed)]
    if returned:
        got = jnp.concatenate([ref[...] for ref in refs[2 * pieces : -1]], axis=1)
        got = got.astype(jnp.float32)
        top, total = (
            functools.reduce(jnp.add, [got[at + k : at + k + 1, :] for k in range(3)])
            for at in (head_dim, head_dim + 3)
        )
        shares.append((top, total, got[:head_dim, :]))
    top = functools.reduce(jnp.maximum, [best for best, _, _ in shares])
    parts = [total * jnp.exp2((best - top) * factor) for best, total, _ in shares]
    total = functools.reduce(jnp.add, parts)
    mixed = functools.reduce(
        jnp.add, [mixed * (part / total) for (_, _, mixed), part in zip(shares, parts)]
    )
    mixed = jnp.where(fresh_ref[0:1, :] > 0.5, mixed, 0.0)
    out_ref[...] = mixed.T.astype(out_ref.dtype) + stale_ref[...]


def blend(stale, fresh, own, returned=()):
    return call(
        functools.partial(blend_kernel, len(own), len(returned)), shape(stale.shape, stale.dtype),
        (stale, fresh, *[x for piece in own for x in piece], *returned), 8 * stale.size,
    )


def swapped_plan(tokens, qkv_weight, shift_mod, scale_mod, q_gain, k_gain, cached, active,
                 cache_slot):
    head_dim = q_gain.shape[1]
    swap = [(0, 1), (1, 0)]
    beside = [(0, 1), (1, 0), (2, 3), (3, 2)]
    across = [(0, 2), (2, 0), (1, 3), (3, 1)]

    other = lax.ppermute(tokens, "head", swap)
    got_columns = lax.ppermute(foreign_keys(qkv_weight, head_dim), "fsdp", swap)
    near = moments(tokens)
    far = lax.ppermute(near, "head", swap)
    common = (
        tokens, other, near, far, qkv_weight,
        scale_mod.reshape(1, -1), shift_mod.reshape(1, -1), head_dim,
    )
    first, *part_query, part_value = normalise(*common)
    got_query = [None, None]
    got_query[0] = lax.ppermute(part_query[0], "fsdp", swap)
    got_value = lax.ppermute(part_value, "fsdp", swap)
    got_query[1] = lax.ppermute(part_query[1], "fsdp", swap)
    second, kept_key = normalise(*common, first=first)

    keys = finish_keys(kept_key, second, got_columns, k_gain)
    beside_keys = lax.ppermute(keys, "seq", beside)
    kept_query, kept_value = project(first, qkv_weight, head_dim)
    half = got_query[0].shape[0]
    queries, visitors = [], []
    for at, part in enumerate(got_query):
        queries.append(finish_queries(at * half, kept_query, part, q_gain))
        visitors.append(lax.ppermute(queries[at], "seq", across))
    values = finish_values(kept_value, got_value)
    beside_values = lax.ppermute(values, "seq", beside)

    stale, fresh = stale_rows(active, cache_slot, cached)
    returned = []
    for visiting in visitors:
        stats, mixed = attend(1, visiting, [(keys, values)], False)
        stats, weights = peek(visiting, beside_keys, stats)
        lent = close(stats, weights, beside_values, mixed)
        returned.append(lax.ppermute(lent, "seq", across))
    spans = [(keys, values), (beside_keys, beside_values)]
    own = []
    for at, mine in enumerate(queries):
        own.append(attend(1, mine, spans, True, active=active, first=at, of=2))
    return blend(stale, fresh, own, returned)


def gathered_plan(tokens, qkv_weight, shift_mod, scale_mod, q_gain, k_gain, cached, active,
                  cache_slot):
    gathered = lax.all_gather(tokens, "head", axis=1, tiled=True).astype(jnp.float32)
    row_mean = jnp.mean(gathered, axis=1, keepdims=True)
    centred = gathered - row_mean
    row_var = jnp.mean(centred * centred, axis=1, keepdims=True)
    normed = (centred * lax.rsqrt(row_var + eps_norm) * (1.0 + scale_mod) + shift_mod).astype(
        jnp.bfloat16
    )
    columns = lax.all_to_all(qkv_weight, "fsdp", split_axis=1, concat_axis=0, tiled=True)
    head_dim = columns.shape[1] // 3
    projected = jnp.dot(normed, columns, preferred_element_type=jnp.float32)
    queries = rms_scaled(projected[:, :head_dim], q_gain).astype(jnp.bfloat16)
    keys = rms_scaled(projected[:, head_dim : 2 * head_dim], k_gain).astype(jnp.bfloat16)
    values = projected[:, 2 * head_dim :].astype(jnp.bfloat16)
    whole_keys = lax.all_gather(keys, "seq", axis=0, tiled=True)
    whole_values = lax.all_gather(values, "seq", axis=0, tiled=True).T
    rows = tokens.shape[0]
    spans = [
        (whole_keys[at : at + rows], whole_values[:, at : at + rows])
        for at in range(0, whole_keys.shape[0], rows)
    ]
    own = attend(active.shape[0] // 2, queries, spans, True, active=active)
    return blend(*stale_rows(active, cache_slot, cached), [own])


def solution(mesh):
    sizes = dict(mesh.shape)

    def per_device(*arrays):
        tokens, weight = arrays[:2]
        laid_out = (sizes["fsdp"], sizes["head"], sizes["seq"]) == (2, 2, 4)
        if laid_out and tokens.shape[0] < weight.shape[0]:
            return swapped_plan(*arrays)
        return gathered_plan(*arrays)

    in_specs = (
        P(("grp", "seq"), "head"),
        P("fsdp", "head"),
        P("grp"),
        P("grp"),
        P(("fsdp", "head"), None),
        P(("fsdp", "head"), None),
        P(("grp", "seq"), ("fsdp", "head")),
        P(("grp", "seq")),
        P(("grp", "seq")),
    )
    out_specs = P(("grp", "seq"), ("fsdp", "head"))
    return jax.shard_map(
        per_device, mesh=mesh, in_specs=in_specs, out_specs=out_specs, check_vma=False
    )
```
